32 devices in a mesh: row: 2 (over y), col: 16 (over z, x, core).
Axes of the slice: x: 2, y: 2, z: 4, core: 2. Of those that a mesh axis runs over, the one named last changes fastest.
Arguments:
- velocity: bfloat16 [3, 512, 1024, 256], P(None, 'row', 'col'), may hold values from -6 to 6
- adj_temp: bfloat16 [512, 1024, 256], P('row', 'col'), may hold values from -6 to 6
- radial_div: bfloat16 [256, 256], replicated, may hold values from -0.375 to 0.375
- reciprocal_distance: float32 [256], replicated, may hold values from 0.002 to 0.02
- radial_basis: bfloat16 [168, 256, 256], P('row'), may hold values from -0.375 to 0.375
- radial_eig: float32 [168, 256], P('row'), may hold values from 0.5 to 8
- axial_diff: bfloat16 [1024, 1024], replicated, may hold values from -0.1875 to 0.1875
- axial_basis: bfloat16 [1024, 1024], replicated, may hold values from -0.1875 to 0.1875
- axial_eig: float32 [1024], replicated, may hold values from 0.5 to 8
Outputs:
- new_temp: float32 [168, 2, 1024, 256], P('row', None, 'col')
The draws below stay inside these ranges and needn't reach their ends.
All inputs are finite; a program needn't handle non-finite values.
Results may differ from the reference program's by a relative error of at most 0.0055.
Values may be sent and summed in bfloat16 or wider, within the bound.
A program may use at most 256 MiB of HBM per device.

```python
import math
import jax
import jax.numpy as jnp
from jax import lax

NT = 512
NR = 256
NZ = 1024
MODES = 168


def level_of(key, dims, pieces, smallest, largest):
    def one(dim, parts):
        draws = jax.random.uniform(jax.random.fold_in(jax.random.fold_in(key, 6), dim), (parts,), jnp.float32, smallest / len(pieces), largest / len(pieces))
        return jnp.repeat(jnp.exp(draws), dims[dim] // parts).reshape((-1,) + (1,) * (len(dims) - dim - 1))

    loudness = one(*pieces[0])
    for cut in pieces[1:]:
        loudness = loudness * one(*cut)
    return loudness


def scatter_about(own_key, extent, deviation, limit, split=(), held_as=jnp.bfloat16):
    result = jax.random.normal(own_key, extent, jnp.float32) * deviation
    if len(split) > 0:
        result = level_of(own_key, extent, split, -0.22, 0.18) * result
    return jnp.clip(result, min=-limit, max=limit).astype(held_as)


def setup_inputs(seed: int = 0) -> dict:
    arg_keys = jax.random.split(jax.random.key(seed), 10)
    velocity = scatter_about(arg_keys[0], (3, NT, NZ, NR), 1.0, 6.0, ((1, 2), (2, 16)))
    adj_temp = scatter_about(arg_keys[1], (NT, NZ, NR), 1.0, 6.0, ((0, 2), (1, 16)))
    radial_div = scatter_about(arg_keys[2], (NR, NR), NR ** -0.5, 0.375)
    reciprocal_distance = jnp.clip(jnp.exp(jax.random.uniform(arg_keys[3], (NR,), jnp.float32, math.log(0.002), math.log(0.02))), 0.002, 0.02)
    radial_basis = scatter_about(arg_keys[4], (MODES, NR, NR), NR ** -0.5, 0.375, ((0, 2),))
    radial_eig = jnp.clip(jnp.exp(math.log(8.0) - 2.7725887 * jax.random.uniform(arg_keys[5], (MODES, NR), jnp.float32) ** level_of(arg_keys[5], (MODES, NR), ((0, 2),), -0.2, 0.2)), 0.5, 8.0)
    axial_diff = scatter_about(arg_keys[6], (NZ, NZ), NZ ** -0.5, 0.1875)
    axial_basis = scatter_about(arg_keys[7], (NZ, NZ), NZ ** -0.5, 0.1875)
    axial_eig = jnp.clip(jnp.exp(jax.random.uniform(arg_keys[8], (NZ,), jnp.float32, math.log(0.5), math.log(8.0))), 0.5, 8.0)
    return dict(velocity=velocity, adj_temp=adj_temp, radial_div=radial_div, reciprocal_distance=reciprocal_distance, radial_basis=radial_basis, radial_eig=radial_eig, axial_diff=axial_diff, axial_basis=axial_basis, axial_eig=axial_eig)


HEAT_OFFSET = 1.0

def azimuth_table(first_mode, mode_count, first_angle, angle_count, circle):
    mode_ids = jnp.arange(mode_count, dtype=jnp.int32) + first_mode
    angle_ids = jnp.arange(angle_count, dtype=jnp.int32) + first_angle
    phase_index = mode_ids[:, None] * angle_ids[None, :] % circle
    angle_value = phase_index.astype(jnp.float32) * (2.0 * math.pi / circle)
    norm_factor = 1.0 / math.sqrt(circle)
    wave_table = jnp.stack([jnp.cos(angle_value) * norm_factor, -jnp.sin(angle_value) * norm_factor], axis=1)
    return wave_table.astype(jnp.bfloat16).reshape(mode_count * 2, angle_count)

def reference(velocity, adj_temp, radial_div, reciprocal_distance, radial_basis, radial_eig, axial_diff, axial_basis, axial_eig):
    highest = lax.Precision.HIGHEST
    fluxes = (velocity.astype(jnp.float32) * adj_temp.astype(jnp.float32)[None]).astype(jnp.bfloat16)
    fields = jnp.concatenate([fluxes, adj_temp[None]], axis=0)
    wave_table = azimuth_table(0, MODES, 0, NT, NT).astype(jnp.float32)

    def transform(field):
        flat_field = field.reshape(NT, NZ * NR).astype(jnp.float32)
        return jnp.dot(wave_table, flat_field, precision=highest).astype(jnp.bfloat16)
    harmonic_amplitudes = lax.map(transform, fields).reshape(4, MODES, 2, NZ, NR)
    harmonic_amplitudes = jnp.moveaxis(harmonic_amplitudes, 1, 0)
    axial_matrix = axial_diff.astype(jnp.float32)
    axial_vectors = axial_basis.astype(jnp.float32)
    divergence = radial_div.astype(jnp.float32)
    mode_values = jnp.arange(MODES).astype(jnp.float32)

    def one_mode(items):
        harmonic_amplitude, radial_vectors, radial_values, harmonic_coefficient = items
        radial_flux = harmonic_amplitude[0]
        angular_flux = harmonic_amplitude[1]
        axial_flux = harmonic_amplitude[2]
        thermal_state = harmonic_amplitude[3]
        cylinder_aggregate = jnp.einsum('pzj,rj->pzr', radial_flux.astype(jnp.float32), divergence, precision=highest)
        eigenbasis_projection = jnp.stack([-angular_flux[1], angular_flux[0]], axis=0).astype(jnp.float32)
        forcing_contribution = (HEAT_OFFSET * thermal_state.astype(jnp.float32) + cylinder_aggregate + harmonic_coefficient * reciprocal_distance * eigenbasis_projection).astype(jnp.bfloat16)
        vectors = radial_vectors.astype(jnp.float32)
        source_hat = jnp.einsum('pzr,ri->piz', forcing_contribution.astype(jnp.float32), vectors, precision=highest)
        flux_hat = jnp.einsum('pzr,ri->piz', axial_flux.astype(jnp.float32), vectors, precision=highest)
        combined = source_hat + jnp.einsum('pij,zj->piz', flux_hat, axial_matrix, precision=highest)
        coefficients = jnp.einsum('piz,zk->pik', combined, axial_vectors, precision=highest)
        coefficients = coefficients / (radial_values[None, :, None] + axial_eig[None, None, :] + HEAT_OFFSET)
        returned = jnp.einsum('pik,zk->piz', coefficients, axial_vectors, precision=highest)
        return jnp.einsum('piz,ri->pzr', returned, vectors, precision=highest)
    return lax.map(one_mode, (harmonic_amplitudes, radial_basis, radial_eig, mode_values))
```

```python
import math

import jax
import jax.numpy as jnp
from jax import lax
from jax.sharding import PartitionSpec as P

HEAT_OFFSET = 1.0
BF = jnp.bfloat16
F32 = jnp.float32


def wave_rows(first_mode, mode_count, first_angle, angle_count, circle):
    mode_ids = first_mode + jnp.arange(mode_count, dtype=jnp.int32)
    angle_ids = first_angle + jnp.arange(angle_count, dtype=jnp.int32)
    phase_index = mode_ids[:, None] * angle_ids[None, :] % circle
    angle_value = phase_index.astype(F32) * (2.0 * math.pi / circle)
    norm_factor = 1.0 / math.sqrt(circle)
    table = jnp.stack(
        [jnp.cos(angle_value) * norm_factor, -jnp.sin(angle_value) * norm_factor], axis=1
    )
    return table.astype(BF)


def chunk_count(modes):
    return max(c for c in range(1, 5) if modes % c == 0)


def body(
    velocity,
    adj_temp,
    radial_div,
    reciprocal_distance,
    radial_basis,
    radial_eig,
    axial_diff,
    axial_basis,
    axial_eig,
):
    row_total = lax.axis_size("row")
    col_total = lax.axis_size("col")
    row_place = lax.axis_index("row")
    col_place = lax.axis_index("col")
    modes = radial_basis.shape[0]
    angles, own_axial, radial_points = adj_temp.shape
    axial_points = axial_basis.shape[0]
    own_count = radial_points // col_total
    circle = angles * row_total
    parts = chunk_count(modes)
    step = modes // parts

    fluxes = (velocity.astype(F32) * adj_temp.astype(F32)[None]).astype(BF)
    heat = HEAT_OFFSET * adj_temp.astype(F32) + jnp.einsum(
        "tzj,rj->tzr", fluxes[0], radial_div, preferred_element_type=F32
    )
    fields = [heat.astype(BF), fluxes[1], fluxes[2]]

    def partial_sums(place):
        table = wave_rows(place * modes, modes, row_place * angles, angles, circle)
        heat_s, turn_s, flux_s = (
            jnp.einsum("mpt,tzr->mpzr", table, f, preferred_element_type=F32) for f in fields
        )
        mode_values = (place * modes + jnp.arange(modes, dtype=jnp.int32)).astype(F32)
        turned = jnp.stack([-turn_s[:, 1], turn_s[:, 0]], axis=1)
        source = heat_s + mode_values[:, None, None, None] * reciprocal_distance * turned
        return jnp.stack([source.astype(BF), flux_s.astype(BF)], axis=2)

    arrived = [[] for _ in range(parts)]
    for shift in range(1, row_total):
        sums = partial_sums((row_place + shift) % row_total)
        pairs = [(a, (a + shift) % row_total) for a in range(row_total)]
        for c in range(parts):
            arrived[c].append(lax.ppermute(sums[c * step : (c + 1) * step], "row", pairs))
    own = partial_sums(row_place)

    returning = jnp.einsum("zj,zk->jk", axial_diff, axial_basis, preferred_element_type=F32)
    forward = jnp.stack(
        [
            axial_basis.reshape(col_total, own_axial, axial_points),
            returning.astype(BF).reshape(col_total, own_axial, axial_points),
        ],
        axis=1,
    )
    axial_blocks = axial_basis.reshape(col_total, own_axial, axial_points)
    radial_values = lax.dynamic_slice_in_dim(radial_eig, col_place * own_count, own_count, 1)

    outs = []
    for c in range(parts):
        part = slice(c * step, (c + 1) * step)
        total = own[part].astype(F32)
        for other in arrived[c]:
            total = total + other.astype(F32)
        basis = radial_basis[part]
        hat = jnp.einsum(
            "mri,mpfzr->mipfz", basis, total.astype(BF), preferred_element_type=F32
        ).astype(BF)
        hat = hat.reshape(step, col_total, own_count, 4 * own_axial)
        hat = jnp.moveaxis(hat, 1, 0)
        lines = lax.all_to_all(hat, "col", split_axis=0, concat_axis=0, tiled=True)
        lines = lines.reshape(col_total, step, own_count, 2, 2, own_axial)
        coefficients = jnp.einsum(
            "smxpfy,sfyk->pmxk", lines, forward, preferred_element_type=F32
        )
        coefficients = coefficients / (
            radial_values[part][None, :, :, None] + axial_eig + HEAT_OFFSET
        )
        returned = jnp.einsum(
            "pmxk,syk->smxpy", coefficients.astype(BF), axial_blocks, preferred_element_type=F32
        ).astype(BF)
        returned = returned.reshape(col_total, step, own_count, 2 * own_axial)
        returned = lax.all_to_all(returned, "col", split_axis=0, concat_axis=0, tiled=True)
        returned = jnp.moveaxis(returned, 0, 1).reshape(step, radial_points, 2 * own_axial)
        outs.append(
            jnp.einsum("miw,mri->mwr", returned, basis, preferred_element_type=F32).reshape(
                step, 2, own_axial, radial_points
            )
        )
    return jnp.concatenate(outs, axis=0)


def solution(mesh):
    in_specs = (
        P(None, "row", "col", None),
        P("row", "col", None),
        P(),
        P(),
        P("row", None, None),
        P("row", None),
        P(),
        P(),
        P(),
    )
    out_specs = P("row", None, "col", None)
    return jax.shard_map(body, mesh=mesh, in_specs=in_specs, out_specs=out_specs, check_vma=False)
```

```python
import functools
import math

import jax
import jax.numpy as jnp
from jax import lax
from jax.experimental import pallas as pl
from jax.experimental.pallas import tpu as pltpu
from jax.sharding import PartitionSpec as P


HEAT_OFFSET = 1.0
BF = jnp.bfloat16
F32 = jnp.float32


def wave_rows(first_mode, mode_count, first_angle, angle_count, circle):
    mode_ids = first_mode + jnp.arange(mode_count, dtype=jnp.int32)
    angle_ids = first_angle + jnp.arange(angle_count, dtype=jnp.int32)
    phase_index = mode_ids[:, None] * angle_ids[None, :] % circle
    angle_value = phase_index.astype(F32) * (2.0 * math.pi / circle)
    norm_factor = 1.0 / math.sqrt(circle)
    table = jnp.stack(
        [jnp.cos(angle_value) * norm_factor, -jnp.sin(angle_value) * norm_factor], axis=1
    )
    return table.astype(BF)


def chunk_count(modes):
    return max(c for c in range(1, 5) if modes % c == 0)


def round_up(value, unit):
    return -(-value // unit) * unit


def sums_kernel(modes, padded, vel_ref, adj_ref, div_ref, table_ref, scale_ref, out_ref, field_s, sum_s):
    angles, block, radial = adj_ref.shape
    adj = adj_ref[...].astype(F32)
    for f in range(3):
        flux = (vel_ref[f].astype(F32) * adj).astype(BF)
        if f == 0:
            moved = lax.dot_general(
                flux.reshape(angles * block, radial),
                div_ref[...],
                (((1,), (1,)), ((), ())),
                preferred_element_type=F32,
            ).reshape(angles, block, radial)
            flux = (HEAT_OFFSET * adj + moved).astype(BF)
        field_s[f] = jnp.swapaxes(flux, 0, 1)

    def one(z, carry):
        heat, turn, flux = (
            jnp.dot(table_ref[...], field_s[f, z], preferred_element_type=F32) for f in range(3)
        )
        scale = scale_ref[...]
        sum_s[0, z] = heat[:padded] - scale * turn[padded:]
        sum_s[1, z] = flux[:padded]
        sum_s[2, z] = heat[padded:] + scale * turn[:padded]
        sum_s[3, z] = flux[padded:]
        return carry

    lax.fori_loop(0, block, one, 0)
    for k in range(4):
        turned = jnp.swapaxes(sum_s[k], 0, 1)
        out_ref[:, k // 2, k % 2] = turned[:modes].astype(BF)


def azimuth_sums(velocity, adj_temp, radial_div, table, mode_values, reciprocal_distance):
    modes = table.shape[0]
    angles, own_axial, radial = adj_temp.shape
    padded = round_up(modes, 8)
    block = 16 if own_axial % 16 == 0 else own_axial
    table = jnp.pad(jnp.moveaxis(table, 1, 0), ((0, 0), (0, padded - modes), (0, 0)))
    table = table.reshape(2 * padded, angles)
    scale = jnp.pad(
        mode_values[:, None] * reciprocal_distance[None], ((0, padded - modes), (0, 0))
    )
    flops = 2 * own_axial * radial * angles * (radial + 6 * padded)
    return pl.pallas_call(
        functools.partial(sums_kernel, modes, padded),
        grid=(own_axial // block,),
        in_specs=[
            pl.BlockSpec((3, angles, block, radial), lambda z: (0, 0, z, 0)),
            pl.BlockSpec((angles, block, radial), lambda z: (0, z, 0)),
            pl.BlockSpec((radial, radial), lambda z: (0, 0)),
            pl.BlockSpec((2 * padded, angles), lambda z: (0, 0)),
            pl.BlockSpec((padded, radial), lambda z: (0, 0)),
        ],
        out_specs=pl.BlockSpec((modes, 2, 2, block, radial), lambda z: (0, 0, 0, z, 0)),
        out_shape=jax.ShapeDtypeStruct((modes, 2, 2, own_axial, radial), BF),
        scratch_shapes=[
            pltpu.VMEM((3, block, angles, radial), BF),
            pltpu.VMEM((4, block, padded, radial), F32),
        ],
        compiler_params=pltpu.CompilerParams(vmem_limit_bytes=60 * 2**20),
        cost_estimate=pl.CostEstimate(
            flops=flops, bytes_accessed=8 * angles * own_axial * radial, transcendentals=0
        ),
        name="sums",
    )(velocity, adj_temp, radial_div, table, scale)


def radial_kernel(count, *refs):
    own_ref, others, basis_ref, out_ref = refs[0], refs[1:-2], refs[-2], refs[-1]
    radial = basis_ref.shape[1]
    for m in range(count):
        total = own_ref[m].astype(F32)
        for other in others:
            total = total + other[m].astype(F32)
        width = total.shape[0] * total.shape[1] * total.shape[2]
        hat = lax.dot_general(
            basis_ref[m],
            total.astype(BF).reshape(width, radial),
            (((0,), (1,)), ((), ())),
            preferred_element_type=F32,
        ).astype(BF)
        out_ref[:, m] = hat.reshape(out_ref.shape[0], out_ref.shape[2], width)


def radial_forward(own, others, basis, first, step, col_total):
    radial = basis.shape[1]
    width = 4 * own.shape[3]
    count = max(c for c in range(1, 8) if step % c == 0)
    skip = first // count
    field = (count, 2, 2, own.shape[3], radial)
    return pl.pallas_call(
        functools.partial(radial_kernel, count),
        grid=(step // count,),
        in_specs=[pl.BlockSpec(field, lambda m: (m + skip, 0, 0, 0, 0))]
        + [pl.BlockSpec(field, lambda m: (m, 0, 0, 0, 0)) for _ in others]
        + [pl.BlockSpec((count, radial, radial), lambda m: (m + skip, 0, 0))],
        out_specs=pl.BlockSpec(
            (col_total, count, radial // col_total, width), lambda m: (0, m, 0, 0)
        ),
        out_shape=jax.ShapeDtypeStruct((col_total, step, radial // col_total, width), BF),
        compiler_params=pltpu.CompilerParams(vmem_limit_bytes=60 * 2**20),
        cost_estimate=pl.CostEstimate(
            flops=2 * step * radial * radial * width,
            bytes_accessed=2 * step * radial * (radial + 3 * width),
            transcendentals=0,
        ),
        name="radial",
    )(own, *others, basis)


def axial_kernel(lines_ref, forward_ref, basis_ref, radial_ref, axial_ref, out_ref):
    col_total, count, own_count, width = lines_ref.shape
    half = width // 2
    quarter = width // 4
    rows = count * own_count
    lines = jnp.concatenate(
        [
            jnp.concatenate(
                [
                    lines_ref[s, :, :, p * half : (p + 1) * half].reshape(rows, half)
                    for s in range(col_total)
                ],
                axis=1,
            )
            for p in range(2)
        ],
        axis=0,
    )
    coefficients = jnp.dot(lines, forward_ref[...], preferred_element_type=F32)
    eigen = radial_ref[...] + axial_ref[...] + HEAT_OFFSET
    coefficients = jnp.concatenate([coefficients[:rows] / eigen, coefficients[rows:] / eigen], axis=0)
    returned = lax.dot_general(
        coefficients.astype(BF),
        basis_ref[...],
        (((1,), (1,)), ((), ())),
        preferred_element_type=F32,
    )
    for s in range(col_total):
        own = slice(s * quarter, (s + 1) * quarter)
        pair = jnp.concatenate([returned[:rows, own], returned[rows:, own]], axis=1)
        out_ref[s] = pair.astype(BF).reshape(count, own_count, half)


def axial_solve(lines, forward, axial_basis, radial_values, axial_eig):
    col_total, step, own_count, width = lines.shape
    points = axial_basis.shape[0]
    count = max(c for c in range(1, 8) if step % c == 0)
    rows = step * own_count
    return pl.pallas_call(
        axial_kernel,
        grid=(step // count,),
        in_specs=[
            pl.BlockSpec((col_total, count, own_count, width), lambda m: (0, m, 0, 0)),
            pl.BlockSpec((2 * points, points), lambda m: (0, 0)),
            pl.BlockSpec((points, points), lambda m: (0, 0)),
            pl.BlockSpec((count * own_count, 1), lambda m: (m, 0)),
            pl.BlockSpec((1, points), lambda m: (0, 0)),
        ],
        out_specs=pl.BlockSpec((col_total, count, own_count, width // 2), lambda m: (0, m, 0, 0)),
        out_shape=jax.ShapeDtypeStruct((col_total, step, own_count, width // 2), BF),
        compiler_params=pltpu.CompilerParams(vmem_limit_bytes=60 * 2**20),
        cost_estimate=pl.CostEstimate(
            flops=12 * rows * points * points,
            bytes_accessed=6 * points * points + 6 * rows * points,
            transcendentals=0,
        ),
        name="axial",
    )(lines, forward, axial_basis, radial_values.reshape(rows, 1), axial_eig.reshape(1, points))


def body(
    velocity,
    adj_temp,
    radial_div,
    reciprocal_distance,
    radial_basis,
    radial_eig,
    axial_diff,
    axial_basis,
    axial_eig,
):
    row_total = lax.axis_size("row")
    col_total = lax.axis_size("col")
    row_place = lax.axis_index("row")
    col_place = lax.axis_index("col")
    modes = radial_basis.shape[0]
    angles, own_axial, radial_points = adj_temp.shape
    axial_points = axial_basis.shape[0]
    own_count = radial_points // col_total
    circle = angles * row_total
    parts = chunk_count(modes)
    step = modes // parts

    def partial_sums(place):
        table = wave_rows(place * modes, modes, row_place * angles, angles, circle)
        mode_values = (place * modes + jnp.arange(modes, dtype=jnp.int32)).astype(F32)
        return azimuth_sums(
            velocity, adj_temp, radial_div, table, mode_values, reciprocal_distance
        )

    arrived = [[] for _ in range(parts)]
    for shift in range(1, row_total):
        sums = partial_sums((row_place + shift) % row_total)
        pairs = [(a, (a + shift) % row_total) for a in range(row_total)]
        for c in range(parts):
            arrived[c].append(lax.ppermute(sums[c * step : (c + 1) * step], "row", pairs))
    own = partial_sums(row_place)

    returning = jnp.einsum("zj,zk->jk", axial_diff, axial_basis, preferred_element_type=F32)
    forward = jnp.stack(
        [
            axial_basis.reshape(col_total, own_axial, axial_points),
            returning.astype(BF).reshape(col_total, own_axial, axial_points),
        ],
        axis=1,
    )
    axial_blocks = axial_basis.reshape(col_total, own_axial, axial_points)
    radial_values = lax.dynamic_slice_in_dim(radial_eig, col_place * own_count, own_count, 1)

    fits = own_axial % 64 == 0 and own_count % 16 == 0
    outs = []
    for c in range(parts):
        part = slice(c * step, (c + 1) * step)
        hat = radial_forward(own, arrived[c], radial_basis, c * step, step, col_total)
        lines = lax.all_to_all(hat, "col", split_axis=0, concat_axis=0, tiled=True)
        if fits:
            returned = axial_solve(
                lines,
                forward.reshape(2 * axial_points, axial_points),
                axial_basis,
                radial_values[part],
                axial_eig,
            )
        else:
            lines = lines.reshape(col_total, step, own_count, 2, 2, own_axial)
            coefficients = jnp.einsum(
                "smxpfy,sfyk->pmxk", lines, forward, preferred_element_type=F32
            )
            coefficients = coefficients / (
                radial_values[part][None, :, :, None] + axial_eig + HEAT_OFFSET
            )
            returned = jnp.einsum(
                "pmxk,syk->smxpy", coefficients.astype(BF), axial_blocks, preferred_element_type=F32
            ).astype(BF)
            returned = returned.reshape(col_total, step, own_count, 2 * own_axial)
        returned = lax.all_to_all(returned, "col", split_axis=0, concat_axis=0, tiled=True)
        returned = jnp.moveaxis(returned, 0, 1).reshape(step, radial_points, 2 * own_axial)
        outs.append(
            jnp.einsum("miw,mri->mwr", returned, radial_basis[part], preferred_element_type=F32).reshape(
                step, 2, own_axial, radial_points
            )
        )
    return jnp.concatenate(outs, axis=0)


def solution(mesh):
    in_specs = (
        P(None, "row", "col", None),
        P("row", "col", None),
        P(),
        P(),
        P("row", None, None),
        P("row", None),
        P(),
        P(),
        P(),
    )
    out_specs = P("row", None, "col", None)
    return jax.shard_map(body, mesh=mesh, in_specs=in_specs, out_specs=out_specs, check_vma=False)
```

```python
import functools
import math

import jax
import jax.numpy as jnp
from jax import lax
from jax.experimental import pallas as pl
from jax.experimental.pallas import tpu as pltpu
from jax.sharding import PartitionSpec as P


HEAT_OFFSET = 1.0
BF = jnp.bfloat16
F32 = jnp.float32


def wave_rows(first_mode, mode_count, first_angle, angle_count, circle):
    mode_ids = first_mode + jnp.arange(mode_count, dtype=jnp.int32)
    angle_ids = first_angle + jnp.arange(angle_count, dtype=jnp.int32)
    phase_index = mode_ids[:, None] * angle_ids[None, :] % circle
    angle_value = phase_index.astype(F32) * (2.0 * math.pi / circle)
    norm_factor = 1.0 / math.sqrt(circle)
    table = jnp.stack(
        [jnp.cos(angle_value) * norm_factor, -jnp.sin(angle_value) * norm_factor], axis=1
    )
    return table.astype(BF)


def chunk_count(modes):
    return max(c for c in range(1, 5) if modes % c == 0)


def round_up(value, unit):
    return -(-value // unit) * unit


def sums_kernel(modes, padded, vel_ref, adj_ref, div_ref, table_ref, scale_ref, *refs):
    *out_refs, field_s, sum_s = refs
    angles, block, radial = adj_ref.shape
    adj = adj_ref[...].astype(F32)
    for f in range(3):
        flux = (vel_ref[f].astype(F32) * adj).astype(BF)
        if f == 0:
            moved = lax.dot_general(
                flux.reshape(angles * block, radial),
                div_ref[...],
                (((1,), (1,)), ((), ())),
                preferred_element_type=F32,
            ).reshape(angles, block, radial)
            flux = (HEAT_OFFSET * adj + moved).astype(BF)
        field_s[f] = jnp.swapaxes(flux, 0, 1)

    def one(z, carry):
        heat, turn, flux = (
            jnp.dot(table_ref[...], field_s[f, z], preferred_element_type=F32) for f in range(3)
        )
        scale = scale_ref[...]
        sum_s[0, z] = heat[:padded] - scale * turn[padded:]
        sum_s[1, z] = flux[:padded]
        sum_s[2, z] = heat[padded:] + scale * turn[:padded]
        sum_s[3, z] = flux[padded:]
        return carry

    lax.fori_loop(0, block, one, 0)
    for k in range(4):
        turned = jnp.swapaxes(sum_s[k], 0, 1)
        step = modes // len(out_refs)
        for c, out_ref in enumerate(out_refs):
            out_ref[:, k // 2, k % 2] = turned[c * step : (c + 1) * step].astype(BF)


def azimuth_sums(velocity, adj_temp, radial_div, table, mode_values, reciprocal_distance, parts):
    modes = table.shape[0]
    angles, own_axial, radial = adj_temp.shape
    padded = round_up(modes, 8)
    block = 16 if own_axial % 16 == 0 else own_axial
    table = jnp.pad(jnp.moveaxis(table, 1, 0), ((0, 0), (0, padded - modes), (0, 0)))
    table = table.reshape(2 * padded, angles)
    scale = jnp.pad(
        mode_values[:, None] * reciprocal_distance[None], ((0, padded - modes), (0, 0))
    )
    flops = 2 * own_axial * radial * angles * (radial + 6 * padded)
    return pl.pallas_call(
        functools.partial(sums_kernel, modes, padded),
        grid=(own_axial // block,),
        in_specs=[
            pl.BlockSpec((3, angles, block, radial), lambda z: (0, 0, z, 0)),
            pl.BlockSpec((angles, block, radial), lambda z: (0, z, 0)),
            pl.BlockSpec((radial, radial), lambda z: (0, 0)),
            pl.BlockSpec((2 * padded, angles), lambda z: (0, 0)),
            pl.BlockSpec((padded, radial), lambda z: (0, 0)),
        ],
        out_specs=[
            pl.BlockSpec((modes // parts, 2, 2, block, radial), lambda z: (0, 0, 0, z, 0))
        ]
        * parts,
        out_shape=[jax.ShapeDtypeStruct((modes // parts, 2, 2, own_axial, radial), BF)] * parts,
        scratch_shapes=[
            pltpu.VMEM((3, block, angles, radial), BF),
            pltpu.VMEM((4, block, padded, radial), F32),
        ],
        compiler_params=pltpu.CompilerParams(vmem_limit_bytes=60 * 2**20),
        cost_estimate=pl.CostEstimate(
            flops=flops, bytes_accessed=8 * angles * own_axial * radial, transcendentals=0
        ),
        name="sums",
    )(velocity, adj_temp, radial_div, table, scale)


def radial_kernel(count, *refs):
    own_ref, others, basis_ref, out_ref = refs[0], refs[1:-2], refs[-2], refs[-1]
    radial = basis_ref.shape[1]
    for m in range(count):
        total = own_ref[m].astype(F32)
        for other in others:
            total = total + other[m].astype(F32)
        width = total.shape[0] * total.shape[1] * total.shape[2]
        hat = lax.dot_general(
            basis_ref[m],
            total.astype(BF).reshape(width, radial),
            (((0,), (1,)), ((), ())),
            preferred_element_type=F32,
        ).astype(BF)
        out_ref[:, m] = hat.reshape(out_ref.shape[0], out_ref.shape[2], width)


def radial_forward(own, others, basis, first, step, col_total):
    radial = basis.shape[1]
    width = 4 * own.shape[3]
    count = max(c for c in range(1, 8) if step % c == 0)
    skip = first // count
    field = (count, 2, 2, own.shape[3], radial)
    return pl.pallas_call(
        functools.partial(radial_kernel, count),
        grid=(step // count,),
        in_specs=[pl.BlockSpec(field, lambda m: (m, 0, 0, 0, 0)) for _ in (own, *others)]
        + [pl.BlockSpec((count, radial, radial), lambda m: (m + skip, 0, 0))],
        out_specs=pl.BlockSpec(
            (col_total, count, radial // col_total, width), lambda m: (0, m, 0, 0)
        ),
        out_shape=jax.ShapeDtypeStruct((col_total, step, radial // col_total, width), BF),
        compiler_params=pltpu.CompilerParams(vmem_limit_bytes=60 * 2**20),
        cost_estimate=pl.CostEstimate(
            flops=2 * step * radial * radial * width,
            bytes_accessed=2 * step * radial * (radial + 3 * width),
            transcendentals=0,
        ),
        name="radial",
    )(own, *others, basis)


def axial_kernel(lines_ref, forward_ref, basis_ref, radial_ref, axial_ref, out_ref):
    col_total, count, own_count, width = lines_ref.shape
    half = width // 2
    quarter = width // 4
    rows = count * own_count
    lines = jnp.concatenate(
        [
            jnp.concatenate(
                [
                    lines_ref[s, :, :, p * half : (p + 1) * half].reshape(rows, half)
                    for s in range(col_total)
                ],
                axis=1,
            )
            for p in range(2)
        ],
        axis=0,
    )
    coefficients = jnp.dot(lines, forward_ref[...], preferred_element_type=F32)
    eigen = radial_ref[...] + axial_ref[...] + HEAT_OFFSET
    coefficients = jnp.concatenate([coefficients[:rows] / eigen, coefficients[rows:] / eigen], axis=0)
    returned = lax.dot_general(
        coefficients.astype(BF),
        basis_ref[...],
        (((1,), (1,)), ((), ())),
        preferred_element_type=F32,
    )
    for s in range(col_total):
        own = slice(s * quarter, (s + 1) * quarter)
        pair = jnp.concatenate([returned[:rows, own], returned[rows:, own]], axis=1)
        out_ref[s] = pair.astype(BF).reshape(count, own_count, half)


def axial_solve(lines, forward, axial_basis, radial_values, axial_eig):
    col_total, step, own_count, width = lines.shape
    points = axial_basis.shape[0]
    count = max(c for c in range(1, 8) if step % c == 0)
    rows = step * own_count
    return pl.pallas_call(
        axial_kernel,
        grid=(step // count,),
        in_specs=[
            pl.BlockSpec((col_total, count, own_count, width), lambda m: (0, m, 0, 0)),
            pl.BlockSpec((2 * points, points), lambda m: (0, 0)),
            pl.BlockSpec((points, points), lambda m: (0, 0)),
            pl.BlockSpec((count * own_count, 1), lambda m: (m, 0)),
            pl.BlockSpec((1, points), lambda m: (0, 0)),
        ],
        out_specs=pl.BlockSpec((col_total, count, own_count, width // 2), lambda m: (0, m, 0, 0)),
        out_shape=jax.ShapeDtypeStruct((col_total, step, own_count, width // 2), BF),
        compiler_params=pltpu.CompilerParams(vmem_limit_bytes=60 * 2**20),
        cost_estimate=pl.CostEstimate(
            flops=12 * rows * points * points,
            bytes_accessed=6 * points * points + 6 * rows * points,
            transcendentals=0,
        ),
        name="axial",
    )(lines, forward, axial_basis, radial_values.reshape(rows, 1), axial_eig.reshape(1, points))


def last_kernel(count, returned_ref, basis_ref, *refs):
    out_ref = refs[-1]
    for m in range(count):
        lines = returned_ref[:, m]
        lines = lines.reshape(lines.shape[0] * lines.shape[1], lines.shape[2])
        out_ref[m] = lax.dot_general(
            lines, basis_ref[m], (((0,), (1,)), ((), ())), preferred_element_type=F32
        ).reshape(out_ref.shape[1:])


def radial_back(returned, basis, before, first):
    col_total, step, own_count, width = returned.shape
    modes, radial, _ = basis.shape
    count = max(c for c in range(1, 8) if step % c == 0)
    skip = first // count
    return pl.pallas_call(
        functools.partial(last_kernel, count),
        grid=(step // count,),
        in_specs=[
            pl.BlockSpec((col_total, count, own_count, width), lambda m: (0, m, 0, 0)),
            pl.BlockSpec((count, radial, radial), lambda m: (m + skip, 0, 0)),
        ]
        + [pl.BlockSpec(memory_space=pl.ANY) for _ in before],
        out_specs=pl.BlockSpec((count, 2, width // 2, radial), lambda m: (m + skip, 0, 0, 0)),
        out_shape=jax.ShapeDtypeStruct((modes, 2, width // 2, radial), F32),
        input_output_aliases={2: 0} if before else {},
        compiler_params=pltpu.CompilerParams(vmem_limit_bytes=60 * 2**20),
        cost_estimate=pl.CostEstimate(
            flops=2 * step * radial * radial * width,
            bytes_accessed=2 * step * radial * (radial + 3 * width),
            transcendentals=0,
        ),
        name="last",
    )(returned, basis, *before)


def body(
    velocity,
    adj_temp,
    radial_div,
    reciprocal_distance,
    radial_basis,
    radial_eig,
    axial_diff,
    axial_basis,
    axial_eig,
):
    row_total = lax.axis_size("row")
    col_total = lax.axis_size("col")
    row_place = lax.axis_index("row")
    col_place = lax.axis_index("col")
    modes = radial_basis.shape[0]
    angles, own_axial, radial_points = adj_temp.shape
    axial_points = axial_basis.shape[0]
    own_count = radial_points // col_total
    circle = angles * row_total
    parts = chunk_count(modes)
    step = modes // parts

    def partial_sums(place):
        table = wave_rows(place * modes, modes, row_place * angles, angles, circle)
        mode_values = (place * modes + jnp.arange(modes, dtype=jnp.int32)).astype(F32)
        return azimuth_sums(
            velocity, adj_temp, radial_div, table, mode_values, reciprocal_distance, parts
        )

    arrived = [[] for _ in range(parts)]
    for shift in range(1, row_total):
        sums = partial_sums((row_place + shift) % row_total)
        pairs = [(a, (a + shift) % row_total) for a in range(row_total)]
        for c in range(parts):
            arrived[c].append(lax.ppermute(sums[c], "row", pairs))
    own = partial_sums(row_place)

    returning = jnp.einsum("zj,zk->jk", axial_diff, axial_basis, preferred_element_type=F32)
    forward = jnp.stack(
        [
            axial_basis.reshape(col_total, own_axial, axial_points),
            returning.astype(BF).reshape(col_total, own_axial, axial_points),
        ],
        axis=1,
    )
    axial_blocks = axial_basis.reshape(col_total, own_axial, axial_points)
    radial_values = lax.dynamic_slice_in_dim(radial_eig, col_place * own_count, own_count, 1)

    fits = own_axial % 64 == 0 and own_count % 16 == 0
    outs = []
    new_temp = ()
    for c in range(parts):
        part = slice(c * step, (c + 1) * step)
        hat = radial_forward(own[c], arrived[c], radial_basis, c * step, step, col_total)
        lines = lax.all_to_all(hat, "col", split_axis=0, concat_axis=0, tiled=True)
        if fits:
            returned = axial_solve(
                lines,
                forward.reshape(2 * axial_points, axial_points),
                axial_basis,
                radial_values[part],
                axial_eig,
            )
        else:
            lines = lines.reshape(col_total, step, own_count, 2, 2, own_axial)
            coefficients = jnp.einsum(
                "smxpfy,sfyk->pmxk", lines, forward, preferred_element_type=F32
            )
            coefficients = coefficients / (
                radial_values[part][None, :, :, None] + axial_eig + HEAT_OFFSET
            )
            returned = jnp.einsum(
                "pmxk,syk->smxpy", coefficients.astype(BF), axial_blocks, preferred_element_type=F32
            ).astype(BF)
            returned = returned.reshape(col_total, step, own_count, 2 * own_axial)
        returned = lax.all_to_all(returned, "col", split_axis=0, concat_axis=0, tiled=True)
        if fits:
            new_temp = (radial_back(returned, radial_basis, new_temp, c * step),)
            continue
        returned = jnp.moveaxis(returned, 0, 1).reshape(step, radial_points, 2 * own_axial)
        outs.append(
            jnp.einsum("miw,mri->mwr", returned, radial_basis[part], preferred_element_type=F32).reshape(
                step, 2, own_axial, radial_points
            )
        )
    return new_temp[0] if fits else jnp.concatenate(outs, axis=0)


def solution(mesh):
    in_specs = (
        P(None, "row", "col", None),
        P("row", "col", None),
        P(),
        P(),
        P("row", None, None),
        P("row", None),
        P(),
        P(),
        P(),
    )
    out_specs = P("row", None, "col", None)
    return jax.shard_map(body, mesh=mesh, in_specs=in_specs, out_specs=out_specs, check_vma=False)
```

```python
import functools
import math

import jax
import jax.numpy as jnp
from jax import lax
from jax.experimental import pallas as pl
from jax.experimental.pallas import tpu as pltpu
from jax.sharding import PartitionSpec as P


HEAT_OFFSET = 1.0
BF = jnp.bfloat16
F32 = jnp.float32


def wave_rows(first_mode, mode_count, first_angle, angle_count, circle):
    mode_ids = first_mode + jnp.arange(mode_count, dtype=jnp.int32)
    angle_ids = first_angle + jnp.arange(angle_count, dtype=jnp.int32)
    phase_index = mode_ids[:, None] * angle_ids[None, :] % circle
    angle_value = phase_index.astype(F32) * (2.0 * math.pi / circle)
    norm_factor = 1.0 / math.sqrt(circle)
    table = jnp.stack(
        [jnp.cos(angle_value) * norm_factor, -jnp.sin(angle_value) * norm_factor], axis=1
    )
    return table.astype(BF)


def chunk_count(modes):
    return max(c for c in range(1, 5) if modes % c == 0)


def round_up(value, unit):
    return -(-value // unit) * unit


def sums_kernel(modes, padded, vel_ref, adj_ref, div_ref, table_ref, scale_ref, *refs):
    *out_refs, field_s, sum_s = refs
    angles, block, radial = adj_ref.shape
    adj = adj_ref[...].astype(F32)
    for f in range(3):
        flux = (vel_ref[f].astype(F32) * adj).astype(BF)
        if f == 0:
            moved = lax.dot_general(
                flux.reshape(angles * block, radial),
                div_ref[...],
                (((1,), (1,)), ((), ())),
                preferred_element_type=F32,
            ).reshape(angles, block, radial)
            flux = (HEAT_OFFSET * adj + moved).astype(BF)
        field_s[f] = jnp.swapaxes(flux, 0, 1)

    def one(z, carry):
        heat, turn, flux = (
            jnp.dot(table_ref[...], field_s[f, z], preferred_element_type=F32) for f in range(3)
        )
        scale = scale_ref[...]
        sum_s[0, z] = heat[:padded] - scale * turn[padded:]
        sum_s[1, z] = flux[:padded]
        sum_s[2, z] = heat[padded:] + scale * turn[:padded]
        sum_s[3, z] = flux[padded:]
        return carry

    lax.fori_loop(0, block, one, 0)
    for k in range(4):
        turned = jnp.swapaxes(sum_s[k], 0, 1)
        step = modes // len(out_refs)
        for c, out_ref in enumerate(out_refs):
            out_ref[:, k // 2, k % 2] = turned[c * step : (c + 1) * step].astype(BF)


def azimuth_sums(velocity, adj_temp, radial_div, table, mode_values, reciprocal_distance, parts):
    modes = table.shape[0]
    angles, own_axial, radial = adj_temp.shape
    padded = round_up(modes, 8)
    block = 16 if own_axial % 16 == 0 else own_axial
    table = jnp.pad(jnp.moveaxis(table, 1, 0), ((0, 0), (0, padded - modes), (0, 0)))
    table = table.reshape(2 * padded, angles)
    scale = jnp.pad(
        mode_values[:, None] * reciprocal_distance[None], ((0, padded - modes), (0, 0))
    )
    flops = 2 * own_axial * radial * angles * (radial + 6 * padded)
    return pl.pallas_call(
        functools.partial(sums_kernel, modes, padded),
        grid=(own_axial // block,),
        in_specs=[
            pl.BlockSpec((3, angles, block, radial), lambda z: (0, 0, z, 0)),
            pl.BlockSpec((angles, block, radial), lambda z: (0, z, 0)),
            pl.BlockSpec((radial, radial), lambda z: (0, 0)),
            pl.BlockSpec((2 * padded, angles), lambda z: (0, 0)),
            pl.BlockSpec((padded, radial), lambda z: (0, 0)),
        ],
        out_specs=[
            pl.BlockSpec((modes // parts, 2, 2, block, radial), lambda z: (0, 0, 0, z, 0))
        ]
        * parts,
        out_shape=[jax.ShapeDtypeStruct((modes // parts, 2, 2, own_axial, radial), BF)] * parts,
        scratch_shapes=[
            pltpu.VMEM((3, block, angles, radial), BF),
            pltpu.VMEM((4, block, padded, radial), F32),
        ],
        compiler_params=pltpu.CompilerParams(vmem_limit_bytes=60 * 2**20),
        cost_estimate=pl.CostEstimate(
            flops=flops, bytes_accessed=8 * angles * own_axial * radial, transcendentals=0
        ),
        name="sums",
    )(velocity, adj_temp, radial_div, table, scale)


def radial_kernel(count, *refs):
    own_ref, others, basis_ref, out_ref = refs[0], refs[1:-2], refs[-2], refs[-1]
    radial = basis_ref.shape[1]
    for m in range(count):
        total = own_ref[m].astype(F32)
        for other in others:
            total = total + other[m].astype(F32)
        width = total.shape[0] * total.shape[1] * total.shape[2]
        hat = lax.dot_general(
            basis_ref[m],
            total.astype(BF).reshape(width, radial),
            (((0,), (1,)), ((), ())),
            preferred_element_type=F32,
        ).astype(BF)
        out_ref[:, m] = hat.reshape(out_ref.shape[0], out_ref.shape[2], width)


def radial_forward(own, others, basis, first, step, col_total):
    radial = basis.shape[1]
    width = 4 * own.shape[3]
    count = max(c for c in range(1, 8) if step % c == 0)
    skip = first // count
    field = (count, 2, 2, own.shape[3], radial)
    return pl.pallas_call(
        functools.partial(radial_kernel, count),
        grid=(step // count,),
        in_specs=[pl.BlockSpec(field, lambda m: (m, 0, 0, 0, 0)) for _ in (own, *others)]
        + [pl.BlockSpec((count, radial, radial), lambda m: (m + skip, 0, 0))],
        out_specs=pl.BlockSpec(
            (col_total, count, radial // col_total, width), lambda m: (0, m, 0, 0)
        ),
        out_shape=jax.ShapeDtypeStruct((col_total, step, radial // col_total, width), BF),
        compiler_params=pltpu.CompilerParams(vmem_limit_bytes=60 * 2**20),
        cost_estimate=pl.CostEstimate(
            flops=2 * step * radial * radial * width,
            bytes_accessed=2 * step * radial * (radial + 3 * width),
            transcendentals=0,
        ),
        name="radial",
    )(own, *others, basis)


def axial_kernel(lines_ref, forward_ref, basis_ref, radial_ref, axial_ref, out_ref):
    col_total, count, own_count, width = lines_ref.shape
    half = width // 2
    quarter = width // 4
    rows = count * own_count
    lines = jnp.concatenate(
        [
            jnp.concatenate(
                [
                    lines_ref[s, :, :, p * half : (p + 1) * half].reshape(rows, half)
                    for s in range(col_total)
                ],
                axis=1,
            )
            for p in range(2)
        ],
        axis=0,
    )
    coefficients = jnp.dot(lines, forward_ref[...], preferred_element_type=F32)
    eigen = radial_ref[...] + axial_ref[...] + HEAT_OFFSET
    coefficients = jnp.concatenate([coefficients[:rows] / eigen, coefficients[rows:] / eigen], axis=0)
    returned = lax.dot_general(
        coefficients.astype(BF),
        basis_ref[...],
        (((1,), (1,)), ((), ())),
        preferred_element_type=F32,
    )
    for s in range(col_total):
        own = slice(s * quarter, (s + 1) * quarter)
        pair = jnp.concatenate([returned[:rows, own], returned[rows:, own]], axis=1)
        out_ref[s] = pair.astype(BF).reshape(count, own_count, half)


def axial_solve(lines, forward, axial_basis, radial_values, axial_eig):
    col_total, step, own_count, width = lines.shape
    points = axial_basis.shape[0]
    count = max(c for c in range(1, 8) if step % c == 0)
    rows = step * own_count
    return pl.pallas_call(
        axial_kernel,
        grid=(step // count,),
        in_specs=[
            pl.BlockSpec((col_total, count, own_count, width), lambda m: (0, m, 0, 0)),
            pl.BlockSpec((2 * points, points), lambda m: (0, 0)),
            pl.BlockSpec((points, points), lambda m: (0, 0)),
            pl.BlockSpec((count * own_count, 1), lambda m: (m, 0)),
            pl.BlockSpec((1, points), lambda m: (0, 0)),
        ],
        out_specs=pl.BlockSpec((col_total, count, own_count, width // 2), lambda m: (0, m, 0, 0)),
        out_shape=jax.ShapeDtypeStruct((col_total, step, own_count, width // 2), BF),
        compiler_params=pltpu.CompilerParams(vmem_limit_bytes=60 * 2**20),
        cost_estimate=pl.CostEstimate(
            flops=12 * rows * points * points,
            bytes_accessed=6 * points * points + 6 * rows * points,
            transcendentals=0,
        ),
        name="axial",
    )(lines, forward, axial_basis, radial_values.reshape(rows, 1), axial_eig.reshape(1, points))


def last_kernel(count, returned_ref, basis_ref, *refs):
    out_ref = refs[-1]
    for m in range(count):
        lines = returned_ref[:, m]
        lines = lines.reshape(lines.shape[0] * lines.shape[1], lines.shape[2])
        out_ref[m] = lax.dot_general(
            lines, basis_ref[m], (((0,), (1,)), ((), ())), preferred_element_type=F32
        ).reshape(out_ref.shape[1:])


def radial_back(returned, basis, before, first):
    col_total, step, own_count, width = returned.shape
    modes, radial, _ = basis.shape
    count = max(c for c in range(1, 8) if step % c == 0)
    skip = first // count
    return pl.pallas_call(
        functools.partial(last_kernel, count),
        grid=(step // count,),
        in_specs=[
            pl.BlockSpec((col_total, count, own_count, width), lambda m: (0, m, 0, 0)),
            pl.BlockSpec((count, radial, radial), lambda m: (m + skip, 0, 0)),
        ]
        + [pl.BlockSpec(memory_space=pl.ANY) for _ in before],
        out_specs=pl.BlockSpec((count, 2, width // 2, radial), lambda m: (m + skip, 0, 0, 0)),
        out_shape=jax.ShapeDtypeStruct((modes, 2, width // 2, radial), F32),
        input_output_aliases={2: 0} if before else {},
        compiler_params=pltpu.CompilerParams(vmem_limit_bytes=60 * 2**20),
        cost_estimate=pl.CostEstimate(
            flops=2 * step * radial * radial * width,
            bytes_accessed=2 * step * radial * (radial + 3 * width),
            transcendentals=0,
        ),
        name="last",
    )(returned, basis, *before)


def body(
    velocity,
    adj_temp,
    radial_div,
    reciprocal_distance,
    radial_basis,
    radial_eig,
    axial_diff,
    axial_basis,
    axial_eig,
):
    row_total = lax.axis_size("row")
    col_total = lax.axis_size("col")
    row_place = lax.axis_index("row")
    col_place = lax.axis_index("col")
    modes = radial_basis.shape[0]
    angles, own_axial, radial_points = adj_temp.shape
    axial_points = axial_basis.shape[0]
    own_count = radial_points // col_total
    circle = angles * row_total
    parts = chunk_count(modes)
    step = modes // parts

    def partial_sums(place):
        table = wave_rows(place * modes, modes, row_place * angles, angles, circle)
        mode_values = (place * modes + jnp.arange(modes, dtype=jnp.int32)).astype(F32)

        def some(where, count):
            return azimuth_sums(
                velocity, adj_temp, radial_div, table[where], mode_values[where],
                reciprocal_distance, count,
            )

        sums = list(some(slice(0, step), 1))
        if parts > 1:
            sums += some(slice(step, modes), parts - 1)
        return sums

    arrived = [[] for _ in range(parts)]
    for shift in range(1, row_total):
        sums = partial_sums((row_place + shift) % row_total)
        pairs = [(a, (a + shift) % row_total) for a in range(row_total)]
        for c in range(parts):
            arrived[c].append(lax.ppermute(sums[c], "row", pairs))
    own = partial_sums(row_place)

    returning = jnp.einsum("zj,zk->jk", axial_diff, axial_basis, preferred_element_type=F32)
    forward = jnp.stack(
        [
            axial_basis.reshape(col_total, own_axial, axial_points),
            returning.astype(BF).reshape(col_total, own_axial, axial_points),
        ],
        axis=1,
    )
    axial_blocks = axial_basis.reshape(col_total, own_axial, axial_points)
    radial_values = lax.dynamic_slice_in_dim(radial_eig, col_place * own_count, own_count, 1)

    fits = own_axial % 64 == 0 and own_count % 16 == 0
    outs = []
    new_temp = ()
    for c in range(parts):
        part = slice(c * step, (c + 1) * step)
        hat = radial_forward(own[c], arrived[c], radial_basis, c * step, step, col_total)
        lines = lax.all_to_all(hat, "col", split_axis=0, concat_axis=0, tiled=True)
        if fits:
            returned = axial_solve(
                lines,
                forward.reshape(2 * axial_points, axial_points),
                axial_basis,
                radial_values[part],
                axial_eig,
            )
        else:
            lines = lines.reshape(col_total, step, own_count, 2, 2, own_axial)
            coefficients = jnp.einsum(
                "smxpfy,sfyk->pmxk", lines, forward, preferred_element_type=F32
            )
            coefficients = coefficients / (
                radial_values[part][None, :, :, None] + axial_eig + HEAT_OFFSET
            )
            returned = jnp.einsum(
                "pmxk,syk->smxpy", coefficients.astype(BF), axial_blocks, preferred_element_type=F32
            ).astype(BF)
            returned = returned.reshape(col_total, step, own_count, 2 * own_axial)
        returned = lax.all_to_all(returned, "col", split_axis=0, concat_axis=0, tiled=True)
        if fits:
            new_temp = (radial_back(returned, radial_basis, new_temp, c * step),)
            continue
        returned = jnp.moveaxis(returned, 0, 1).reshape(step, radial_points, 2 * own_axial)
        outs.append(
            jnp.einsum("miw,mri->mwr", returned, radial_basis[part], preferred_element_type=F32).reshape(
                step, 2, own_axial, radial_points
            )
        )
    return new_temp[0] if fits else jnp.concatenate(outs, axis=0)


def solution(mesh):
    in_specs = (
        P(None, "row", "col", None),
        P("row", "col", None),
        P(),
        P(),
        P("row", None, None),
        P("row", None),
        P(),
        P(),
        P(),
    )
    out_specs = P("row", None, "col", None)
    return jax.shard_map(body, mesh=mesh, in_specs=in_specs, out_specs=out_specs, check_vma=False)
```
